32 devices in a mesh: row: 4 (over x, core), col: 8 (over z, y).
Axes of the slice: x: 2, y: 2, z: 4, core: 2. Of those that a mesh axis runs over, the one named last changes fastest.
Arguments:
- particles: float32 [12, 4096], P(None, ('row', 'col')), may hold values from -6 to 6
- masses: float32 [4096], P(('row', 'col')), may hold values from 0.2 to 5
- levels: int32 [32], P(('row', 'col')), may hold values from 0 to 3, as said below
- counts: int32 [32], P(('row', 'col')), may hold values from 64 to 128, as said below
- active_order: int32 [32, 128], P(('row', 'col')), may hold values from 0 to 127, each once within a row
Outputs:
- advanced: float32 [12, 4096], P(None, ('row', 'col'))
The draws below stay inside these ranges and needn't reach their ends.
Inputs may be any that keep to these rules, and one draw needn't show every extreme that they name: A block whose level is 0 takes part in both substeps, level 1 only in the second, higher levels in neither. `counts`: 128 is reached in every draw. `active_order`: each row holds every number of 0 to 127 once.
All inputs are finite; a program needn't handle non-finite values.
Results may differ from the reference program's by a relative error of at most 0.0003.
Values sent between devices are 32-bit elements; how exact they have to be, the bound alone decides.
A program may use at most 64 MiB of HBM per device.

```python
import math
import jax
import jax.numpy as jnp
from jax import lax

BLOCK = 128
PARTICLES = 4096
BLOCKS = 32
ROW_BLOCKS = 8


def draw_levels(key, part):
    row_key, block_key, pick_key = jax.random.split(jax.random.fold_in(key, 11), 3)
    row_total = BLOCKS // ROW_BLOCKS
    heat_level = jax.random.randint(row_key, (row_total,), 0, 3)
    hot_row = jax.random.randint(pick_key, (), 0, row_total)
    heat_level = heat_level.at[hot_row].set(0)
    row_of = jnp.arange(BLOCKS, dtype=jnp.int32) // ROW_BLOCKS
    span_size = 2 + 2 * heat_level[row_of]
    raw_draw = jax.random.randint(block_key, (BLOCKS,), 0, 1 << 30) % span_size
    levels = jnp.minimum(raw_draw, 3)
    first_block = hot_row * ROW_BLOCKS
    levels = levels.at[first_block].set(0).at[first_block + 1].set(3)
    return levels.astype(jnp.int32)


def draw_counts(key, part):
    value_key, pick_key = jax.random.split(jax.random.fold_in(key, 23))
    drawn = jax.random.randint(value_key, (BLOCKS,), BLOCK // 2, BLOCK + 1)
    picked = jax.random.randint(pick_key, (), 0, BLOCKS)
    drawn = drawn.at[picked].set(BLOCK)
    return drawn.astype(jnp.int32)


def block_levels(key, extent, pieces, low, high):
    factor_of, own = 1.0, jax.random.fold_in(key, 6)
    for dim, blocks in pieces:
        draws = jnp.exp(jax.random.uniform(jax.random.fold_in(own, dim), (blocks,), jnp.float32, low / len(pieces), high / len(pieces)))
        factor_of = factor_of * jnp.repeat(draws, extent[dim] // blocks).reshape([-1 if axis == dim else 1 for axis in range(len(extent))])
    return factor_of


def scatter_about(rng, shape, scale, bound, pieces=(), kind=jnp.bfloat16):
    values = jax.random.normal(rng, shape, jnp.float32) * scale
    if len(pieces) > 0:
        values = block_levels(rng, shape, pieces, -0.22, 0.18) * values
    return jnp.clip(values, min=-bound, max=bound).astype(kind)


def setup_inputs(seed: int = 0) -> dict:
    key_of = jax.random.split(jax.random.key(seed), 6)
    particles = scatter_about(key_of[0], (12, PARTICLES), 1.0, 6.0, ((1, 32),), jnp.float32)
    masses = jnp.clip(jnp.exp(math.log(5.0) - 3.218876 * jax.random.uniform(key_of[1], (PARTICLES,), jnp.float32) ** block_levels(key_of[1], (PARTICLES,), ((0, 32),), -0.2, 0.2)), 0.2, 5.0)
    levels = draw_levels(jax.random.fold_in(key_of[5], 71), 0)
    counts = draw_counts(jax.random.fold_in(key_of[5], 71), 0)
    active_order = jax.vmap(lambda own: jax.random.permutation(own, BLOCK))(jax.random.split(key_of[4], BLOCKS)).reshape((BLOCKS, BLOCK)).astype(jnp.int32)
    return dict(particles=particles, masses=masses, levels=levels, counts=counts, active_order=active_order)


step_time = 0.5
soft_coef = 1.5

def listed_mask(counts, active_order):
    slot_ids = jnp.arange(active_order.shape[1], dtype=jnp.int32)
    listed = (active_order[:, :, None] == slot_ids[None, None, :]) & (slot_ids[None, :, None] < counts[:, None, None])
    return jnp.any(listed, axis=1)

def predict_rows(state, scaled, elapsed):
    position, velocity = (state[0:3], state[3:6])
    acceleration, jerk_old = (state[6:9], state[9:12])
    pred_pos = position + velocity * elapsed + acceleration * (elapsed * elapsed / 2.0) + jerk_old * (elapsed * elapsed * elapsed / 6.0)
    pred_vel = velocity + acceleration * elapsed + jerk_old * (elapsed * elapsed / 2.0)
    return jnp.concatenate([pred_pos, pred_vel, scaled[None, :]], axis=0)

def corrected(state, forces, elapsed):
    position, velocity = (state[0:3], state[3:6])
    acceleration, jerk_old = (state[6:9], state[9:12])
    new_acc, new_jerk = (forces[0:3], forces[3:6])
    half_step = elapsed / 2.0
    twelfth = elapsed * elapsed / 12.0
    new_vel = velocity + (acceleration + new_acc) * half_step + (jerk_old - new_jerk) * twelfth
    new_pos = position + (velocity + new_vel) * half_step + (acceleration - new_acc) * twelfth
    return jnp.concatenate([new_pos, new_vel, new_acc, new_jerk], axis=0)

def block_forces(target_rows, source_rows, soft_sq):
    offset = [source_rows[axis_id][None, :] - target_rows[axis_id][:, None] for axis_id in range(3)]
    spread = [source_rows[axis_id + 3][None, :] - target_rows[axis_id + 3][:, None] for axis_id in range(3)]
    dist_sq = offset[0] * offset[0] + offset[1] * offset[1] + offset[2] * offset[2] + soft_sq
    inv_sq = 1.0 / dist_sq
    inv_cube = inv_sq * jnp.sqrt(inv_sq)
    radial = 3.0 * (offset[0] * spread[0] + offset[1] * spread[1] + offset[2] * spread[2]) * inv_sq
    kernels = [inv_cube * offset[axis_id] for axis_id in range(3)]
    kernels = kernels + [inv_cube * (spread[axis_id] - radial * offset[axis_id]) for axis_id in range(3)]
    return jnp.stack([lax.optimization_barrier(jnp.sum(kernel * source_rows[6][None, :], axis=1)) for kernel in kernels])

def reference(particles, masses, levels, counts, active_order):
    soft_sq = soft_coef * float(PARTICLES) ** (-2.0 / 3.0)
    scaled = masses * (1.0 / float(PARTICLES))
    chosen = listed_mask(counts, active_order)
    period = jnp.left_shift(jnp.ones_like(levels), levels)
    state = particles
    last_time = jnp.zeros((PARTICLES,), jnp.float32)
    for substep in (1, 2):
        now_time = substep * step_time
        block_on = substep % period == 0
        active = (chosen & block_on[:, None]).reshape(PARTICLES)
        elapsed = now_time - last_time
        predicted = predict_rows(state, scaled, elapsed)

        def one_block(block_id):
            first_col = block_id * BLOCK
            target_rows = lax.dynamic_slice_in_dim(predicted, first_col, BLOCK, 1)

            def compute(unused):
                return block_forces(target_rows, predicted, soft_sq)

            def skipped(unused):
                return jnp.zeros((6, BLOCK), jnp.float32)
            return lax.cond(block_on[block_id], compute, skipped, 0)
        forces = lax.map(one_block, jnp.arange(BLOCKS, dtype=jnp.int32))
        forces = jnp.transpose(forces, (1, 0, 2)).reshape(6, PARTICLES)
        updated = corrected(state, forces, elapsed)
        state = jnp.where(active[None, :], updated, state)
        last_time = jnp.where(active, now_time, last_time)
    return state
```

```python
import functools

import jax
import jax.numpy as jnp
from jax import lax
from jax.experimental import pallas as pl
from jax.experimental.pallas import tpu as pltpu
from jax.sharding import PartitionSpec as P

step_time = 0.5
soft_coef = 1.5
lane_tile = 8
wave = 4
vmem_grant = 16 * 1024 * 1024


def flip(index, mask):
    out = index
    bit = 1
    while bit <= mask:
        if mask & bit:
            out = out + bit * (1 - 2 * ((index // bit) % 2))
        bit *= 2
    return out


def shifted(index, offset, size):
    if size & (size - 1) == 0:
        return flip(index, offset)
    return lax.rem(index + offset, size)


def nearness(pair):
    dr, dc = pair
    return dr // 2 + dc % 2 + dc // 2, dr % 2


def kernel(
    rows, cols, soft_sq, mass_scale,
    part_hbm, mass_hbm, level_hbm, count_hbm, order_hbm, out_ref,
    part, mass, level, count, order, first, second, spread_t, acc,
    in_sem, send_sem, recv_sem,
):
    row, col = lax.axis_index("row"), lax.axis_index("col")
    total = rows * cols
    block = part.shape[1]
    offsets = sorted(
        ((dr, dc) for dr in range(rows) for dc in range(cols)), key=nearness
    )
    peers = [(shifted(row, dr, rows), shifted(col, dc, cols)) for dr, dc in offsets]

    barrier = pltpu.get_barrier_semaphore()
    for peer in peers[:0:-1]:
        pl.semaphore_signal(
            barrier, inc=1, device_id=peer, device_id_type=pl.DeviceIdType.MESH
        )
    loads = [
        pltpu.make_async_copy(src, dst, in_sem.at[i])
        for i, (src, dst) in enumerate(
            (
                (part_hbm, part),
                (mass_hbm, mass),
                (level_hbm, level),
                (count_hbm, count),
                (order_hbm, order),
            )
        )
    ]
    for load in loads:
        load.start()
    for load in loads:
        load.wait()

    def predict(pos, vel, force, jerk, e):
        pred_pos = pos + vel * e + force * (e * e / 2.0) + jerk * (e * e * e / 6.0)
        pred_vel = vel + force * e + jerk * (e * e / 2.0)
        return pred_pos, pred_vel

    def correct(pos, vel, force, jerk, new_force, new_jerk, e):
        half, twelfth = e / 2.0, e * e / 12.0
        new_vel = vel + (force + new_force) * half + (jerk - new_jerk) * twelfth
        new_pos = pos + (vel + new_vel) * half + (force - new_force) * twelfth
        return new_pos, new_vel

    def send(buffer, used, phase):
        copies = []
        for step in range(1, total):
            copy = pltpu.make_async_remote_copy(
                src_ref=buffer.at[0, pl.ds(0, used)],
                dst_ref=buffer.at[step, pl.ds(0, used)],
                send_sem=send_sem.at[phase, step],
                recv_sem=recv_sem.at[phase, step],
                device_id=peers[step],
                device_id_type=pl.DeviceIdType.MESH,
            )
            copy.start()
            copies.append(copy)
        return copies

    def stage_targets(buffer):
        for axis in range(6):
            line = jnp.broadcast_to(buffer[0, axis : axis + 1, :], (block, block))
            spread_t[axis] = jnp.transpose(line)

    def gather_forces(buffer, copies):
        acc[...] = jnp.zeros_like(acc)
        width = wave if total <= 64 else 8
        for lo in range(0, total, width):
            hi = min(lo + width, total)
            for step in range(max(lo, 1), hi):
                copies[step - 1].wait_recv()

            def tile(group, carry):
                at = pl.ds(pl.multiple_of(group * lane_tile, lane_tile), lane_tile)
                here = [spread_t[axis, at, :] for axis in range(6)]
                sums = [acc[axis, at, :] for axis in range(6)]
                for s in range(lo, hi):
                    r = [buffer[s, x : x + 1, :] - here[x] for x in range(3)]
                    w = [buffer[s, x + 3 : x + 4, :] - here[x + 3] for x in range(3)]
                    s2 = (r[0] * r[0] + r[1] * r[1]) + (r[2] * r[2] + soft_sq)
                    inv = lax.rsqrt(s2)
                    inv_sq = inv * inv
                    weight = (first[s, 6:7, :] * inv) * inv_sq
                    radial = ((r[0] * w[0] + r[1] * w[1]) + r[2] * w[2]) * (inv_sq * 3.0)
                    for x in range(3):
                        sums[x] = sums[x] + weight * r[x]
                        sums[x + 3] = sums[x + 3] + weight * (w[x] - radial * r[x])
                for axis in range(6):
                    acc[axis, at, :] = sums[axis]
                return carry

            lax.fori_loop(0, block // lane_tile, tile, 0, unroll=4 if total <= 64 else 1)
        sums = [
            jnp.sum(jnp.transpose(acc[axis]), axis=0, keepdims=True) for axis in range(6)
        ]
        return jnp.concatenate(sums[:3], axis=0), jnp.concatenate(sums[3:], axis=0)

    pos, vel, force, jerk = (part[3 * k : 3 * k + 3, :] for k in range(4))
    pred_pos, pred_vel = predict(pos, vel, force, jerk, step_time)
    first[0, 0:3, :] = pred_pos
    first[0, 3:6, :] = pred_vel
    first[0, 6:7, :] = mass[...] * mass_scale

    pl.semaphore_wait(barrier, total - 1)
    copies = send(first, 7, 0)

    slot = lax.broadcasted_iota(jnp.int32, (1, block), 1)
    kept = jnp.where(slot < count[...], order[...], -1)
    kept = jnp.transpose(jnp.broadcast_to(kept.astype(jnp.float32), (block, block)))
    name = lax.broadcasted_iota(jnp.int32, (block, block), 1).astype(jnp.float32)
    listed = jnp.sum(jnp.where(kept == name, 1.0, 0.0), axis=0, keepdims=True)
    on_first = jnp.where(level[...] == 0, listed, 0.0) > 0.5
    on_second = jnp.where(level[...] <= 1, listed, 0.0) > 0.5

    stage_targets(first)
    new_force, new_jerk = gather_forces(first, copies)
    new_pos, new_vel = correct(pos, vel, force, jerk, new_force, new_jerk, step_time)
    pos = jnp.where(on_first, new_pos, pos)
    vel = jnp.where(on_first, new_vel, vel)
    force = jnp.where(on_first, new_force, force)
    jerk = jnp.where(on_first, new_jerk, jerk)
    elapsed = jnp.where(on_first, step_time, 2.0 * step_time)

    pred_pos, pred_vel = predict(pos, vel, force, jerk, elapsed)
    second[0, 0:3, :] = pred_pos
    second[0, 3:6, :] = pred_vel
    later = send(second, 6, 1)
    stage_targets(second)
    new_force, new_jerk = gather_forces(second, later)
    new_pos, new_vel = correct(pos, vel, force, jerk, new_force, new_jerk, elapsed)
    out_ref[0:3, :] = jnp.where(on_second, new_pos, pos)
    out_ref[3:6, :] = jnp.where(on_second, new_vel, vel)
    out_ref[6:9, :] = jnp.where(on_second, new_force, force)
    out_ref[9:12, :] = jnp.where(on_second, new_jerk, jerk)
    for copy in copies + later:
        copy.wait_send()


def per_device(particles, masses, levels, counts, active_order):
    rows, cols = lax.axis_size("row"), lax.axis_size("col")
    total = rows * cols
    block = particles.shape[1]
    particle_total = block * total
    soft_sq = soft_coef * float(particle_total) ** (-2.0 / 3.0)
    f32 = jnp.float32
    return pl.pallas_call(
        functools.partial(kernel, rows, cols, soft_sq, 1.0 / float(particle_total)),
        out_shape=jax.ShapeDtypeStruct(particles.shape, f32),
        in_specs=[pl.BlockSpec(memory_space=pl.ANY)] * 5,
        out_specs=pl.BlockSpec(memory_space=pltpu.VMEM),
        scratch_shapes=[
            pltpu.VMEM(particles.shape, f32),
            pltpu.VMEM((1, block), f32),
            pltpu.VMEM((1, 1), jnp.int32),
            pltpu.VMEM((1, 1), jnp.int32),
            pltpu.VMEM((1, block), jnp.int32),
            pltpu.VMEM((total, 8, block), f32),
            pltpu.VMEM((total, 8, block), f32),
            pltpu.VMEM((6, block, block), f32),
            pltpu.VMEM((6, block, block), f32),
            pltpu.SemaphoreType.DMA((5,)),
            pltpu.SemaphoreType.DMA((2, total)),
            pltpu.SemaphoreType.DMA((2, total)),
        ],
        compiler_params=pltpu.CompilerParams(
            collective_id=0, has_side_effects=True, vmem_limit_bytes=vmem_grant
        ),
    )(*(pltpu.with_memory_space_constraint(a, pltpu.HBM) for a in (particles, masses.reshape(1, block))), levels.reshape(1, 1), counts.reshape(1, 1), pltpu.with_memory_space_constraint(active_order, pltpu.HBM))


def solution(mesh):
    in_specs = (
        P(None, ("row", "col")),
        P(("row", "col")),
        P(("row", "col")),
        P(("row", "col")),
        P(("row", "col"), None),
    )
    out_specs = P(None, ("row", "col"))
    return jax.shard_map(
        per_device, mesh=mesh, in_specs=in_specs, out_specs=out_specs, check_vma=False
    )
```

```python
import functools

import jax
import jax.numpy as jnp
from jax import lax
from jax.experimental import pallas as pl
from jax.experimental.pallas import tpu as pltpu
from jax.sharding import PartitionSpec as P

step_time = 0.5
soft_coef = 1.5
lane_tile = 8
wave = 2
vmem_grant = 16 * 1024 * 1024


def flip(index, mask):
    out = index
    bit = 1
    while bit <= mask:
        if mask & bit:
            out = out + bit * (1 - 2 * ((index // bit) % 2))
        bit *= 2
    return out


def shifted(index, offset, size):
    if size & (size - 1) == 0:
        return flip(index, offset)
    return lax.rem(index + offset, size)


def nearness(pair):
    dr, dc = pair
    return dr // 2 + dc % 2 + dc // 2, dr % 2


def kernel(
    rows, cols, soft_sq, mass_scale,
    part_hbm, mass_hbm, level_hbm, count_hbm, order_hbm, out_ref,
    part, mass, level, count, order, first, second, spread_t, acc,
    in_sem, send_sem, recv_sem,
):
    row, col = lax.axis_index("row"), lax.axis_index("col")
    total = rows * cols
    block = part.shape[1]
    offsets = sorted(
        ((dr, dc) for dr in range(rows) for dc in range(cols)), key=nearness
    )
    peers = [(shifted(row, dr, rows), shifted(col, dc, cols)) for dr, dc in offsets]

    barrier = pltpu.get_barrier_semaphore()
    for peer in peers[:0:-1]:
        pl.semaphore_signal(
            barrier, inc=1, device_id=peer, device_id_type=pl.DeviceIdType.MESH
        )
    loads = [
        pltpu.make_async_copy(src, dst, in_sem.at[i])
        for i, (src, dst) in enumerate(
            (
                (part_hbm, part),
                (mass_hbm, mass),
                (level_hbm, level),
                (count_hbm, count),
                (order_hbm, order),
            )
        )
    ]
    for load in loads:
        load.start()
    for load in loads:
        load.wait()

    def predict(pos, vel, force, jerk, e):
        pred_pos = pos + vel * e + force * (e * e / 2.0) + jerk * (e * e * e / 6.0)
        pred_vel = vel + force * e + jerk * (e * e / 2.0)
        return pred_pos, pred_vel

    def correct(pos, vel, force, jerk, new_force, new_jerk, e):
        half, twelfth = e / 2.0, e * e / 12.0
        new_vel = vel + (force + new_force) * half + (jerk - new_jerk) * twelfth
        new_pos = pos + (vel + new_vel) * half + (force - new_force) * twelfth
        return new_pos, new_vel

    def send(buffer, used, phase):
        copies = []
        for step in range(1, total):
            copy = pltpu.make_async_remote_copy(
                src_ref=buffer.at[0, pl.ds(0, used)],
                dst_ref=buffer.at[step, pl.ds(0, used)],
                send_sem=send_sem.at[phase, step],
                recv_sem=recv_sem.at[phase, step],
                device_id=peers[step],
                device_id_type=pl.DeviceIdType.MESH,
            )
            copy.start()
            copies.append(copy)
        return copies

    def stage_targets(buffer):
        for axis in range(6):
            line = jnp.broadcast_to(buffer[0, axis : axis + 1, :], (block, block))
            spread_t[axis] = jnp.transpose(line)

    def gather_forces(buffer, copies):
        acc[...] = jnp.zeros_like(acc)
        width = wave if total <= 64 else 8
        for lo in range(0, total, width):
            hi = min(lo + width, total)
            for step in range(max(lo, 1), hi):
                copies[step - 1].wait_recv()

            def tile(group, carry):
                at = pl.ds(pl.multiple_of(group * lane_tile, lane_tile), lane_tile)
                here = [spread_t[axis, at, :] for axis in range(6)]
                sums = [acc[axis, at, :] for axis in range(6)]
                for s in range(lo, hi):
                    r = [buffer[s, x : x + 1, :] - here[x] for x in range(3)]
                    w = [buffer[s, x + 3 : x + 4, :] - here[x + 3] for x in range(3)]
                    s2 = (r[0] * r[0] + r[1] * r[1]) + (r[2] * r[2] + soft_sq)
                    inv = lax.rsqrt(s2)
                    inv_sq = inv * inv
                    weight = (first[s, 6:7, :] * inv) * inv_sq
                    radial = ((r[0] * w[0] + r[1] * w[1]) + r[2] * w[2]) * (inv_sq * 3.0)
                    for x in range(3):
                        sums[x] = sums[x] + weight * r[x]
                        sums[x + 3] = sums[x + 3] + weight * (w[x] - radial * r[x])
                for axis in range(6):
                    acc[axis, at, :] = sums[axis]
                return carry

            lax.fori_loop(0, block // lane_tile, tile, 0, unroll=16 if total <= 64 else 1)
        sums = [
            jnp.sum(jnp.transpose(acc[axis]), axis=0, keepdims=True) for axis in range(6)
        ]
        return jnp.concatenate(sums[:3], axis=0), jnp.concatenate(sums[3:], axis=0)

    pos, vel, force, jerk = (part[3 * k : 3 * k + 3, :] for k in range(4))
    pred_pos, pred_vel = predict(pos, vel, force, jerk, step_time)
    first[0, 0:3, :] = pred_pos
    first[0, 3:6, :] = pred_vel
    first[0, 6:7, :] = mass[...] * mass_scale

    pl.semaphore_wait(barrier, total - 1)
    copies = send(first, 7, 0)

    slot = lax.broadcasted_iota(jnp.int32, (1, block), 1)
    kept = jnp.where(slot < count[...], order[...], -1)
    kept = jnp.transpose(jnp.broadcast_to(kept.astype(jnp.float32), (block, block)))
    name = lax.broadcasted_iota(jnp.int32, (block, block), 1).astype(jnp.float32)
    listed = jnp.sum(jnp.where(kept == name, 1.0, 0.0), axis=0, keepdims=True)
    on_first = jnp.where(level[...] == 0, listed, 0.0) > 0.5
    on_second = jnp.where(level[...] <= 1, listed, 0.0) > 0.5

    stage_targets(first)
    new_force, new_jerk = gather_forces(first, copies)
    new_pos, new_vel = correct(pos, vel, force, jerk, new_force, new_jerk, step_time)
    pos = jnp.where(on_first, new_pos, pos)
    vel = jnp.where(on_first, new_vel, vel)
    force = jnp.where(on_first, new_force, force)
    jerk = jnp.where(on_first, new_jerk, jerk)
    elapsed = jnp.where(on_first, step_time, 2.0 * step_time)

    pred_pos, pred_vel = predict(pos, vel, force, jerk, elapsed)
    second[0, 0:3, :] = pred_pos
    second[0, 3:6, :] = pred_vel
    later = send(second, 6, 1)
    stage_targets(second)
    new_force, new_jerk = gather_forces(second, later)
    new_pos, new_vel = correct(pos, vel, force, jerk, new_force, new_jerk, elapsed)
    out_ref[0:3, :] = jnp.where(on_second, new_pos, pos)
    out_ref[3:6, :] = jnp.where(on_second, new_vel, vel)
    out_ref[6:9, :] = jnp.where(on_second, new_force, force)
    out_ref[9:12, :] = jnp.where(on_second, new_jerk, jerk)
    for copy in copies + later:
        copy.wait_send()


def per_device(particles, masses, levels, counts, active_order):
    rows, cols = lax.axis_size("row"), lax.axis_size("col")
    total = rows * cols
    block = particles.shape[1]
    particle_total = block * total
    soft_sq = soft_coef * float(particle_total) ** (-2.0 / 3.0)
    f32 = jnp.float32
    return pl.pallas_call(
        functools.partial(kernel, rows, cols, soft_sq, 1.0 / float(particle_total)),
        out_shape=jax.ShapeDtypeStruct(particles.shape, f32),
        in_specs=[pl.BlockSpec(memory_space=pl.ANY)] * 5,
        out_specs=pl.BlockSpec(memory_space=pltpu.VMEM),
        scratch_shapes=[
            pltpu.VMEM(particles.shape, f32),
            pltpu.VMEM((1, block), f32),
            pltpu.VMEM((1, 1), jnp.int32),
            pltpu.VMEM((1, 1), jnp.int32),
            pltpu.VMEM((1, block), jnp.int32),
            pltpu.VMEM((total, 8, block), f32),
            pltpu.VMEM((total, 8, block), f32),
            pltpu.VMEM((6, block, block), f32),
            pltpu.VMEM((6, block, block), f32),
            pltpu.SemaphoreType.DMA((5,)),
            pltpu.SemaphoreType.DMA((2, total)),
            pltpu.SemaphoreType.DMA((2, total)),
        ],
        compiler_params=pltpu.CompilerParams(
            collective_id=0, has_side_effects=True, vmem_limit_bytes=vmem_grant
        ),
    )(*(pltpu.with_memory_space_constraint(a, pltpu.HBM) for a in (particles, masses.reshape(1, block))), levels.reshape(1, 1), counts.reshape(1, 1), pltpu.with_memory_space_constraint(active_order, pltpu.HBM))


def solution(mesh):
    in_specs = (
        P(None, ("row", "col")),
        P(("row", "col")),
        P(("row", "col")),
        P(("row", "col")),
        P(("row", "col"), None),
    )
    out_specs = P(None, ("row", "col"))
    return jax.shard_map(
        per_device, mesh=mesh, in_specs=in_specs, out_specs=out_specs, check_vma=False
    )
```

```python
import functools

import jax
import jax.numpy as jnp
from jax import lax
from jax.experimental import pallas as pl
from jax.experimental.pallas import tpu as pltpu
from jax.sharding import PartitionSpec as P

step_time = 0.5
soft_coef = 1.5
lane_tile = 8
wave = 2
vmem_grant = 16 * 1024 * 1024


def flip(index, mask):
    out = index
    bit = 1
    while bit <= mask:
        if mask & bit:
            out = out + bit * (1 - 2 * ((index // bit) % 2))
        bit *= 2
    return out


def shifted(index, offset, size):
    if size & (size - 1) == 0:
        return flip(index, offset)
    return lax.rem(index + offset, size)


def nearness(pair):
    dr, dc = pair
    return dr // 2 + dc % 2 + dc // 2, dr % 2


def kernel(
    rows, cols, soft_sq, mass_scale,
    part_hbm, mass_hbm, level_hbm, count_hbm, order_hbm, out_ref,
    part, mass, level, count, order, first, second, spread_t, acc,
    in_sem, send_sem, recv_sem,
):
    row, col = lax.axis_index("row"), lax.axis_index("col")
    total = rows * cols
    block = part.shape[1]
    offsets = sorted(
        ((dr, dc) for dr in range(rows) for dc in range(cols)), key=nearness
    )
    peers = [(shifted(row, dr, rows), shifted(col, dc, cols)) for dr, dc in offsets]

    loads = [
        pltpu.make_async_copy(src, dst, in_sem.at[i])
        for i, (src, dst) in enumerate(
            (
                (part_hbm, part),
                (mass_hbm, mass),
                (level_hbm, level),
                (count_hbm, count),
                (order_hbm, order),
            )
        )
    ]
    for load in loads:
        load.start()
    barrier = pltpu.get_barrier_semaphore()
    for peer in peers[:0:-1]:
        pl.semaphore_signal(
            barrier, inc=1, device_id=peer, device_id_type=pl.DeviceIdType.MESH
        )
    for load in loads:
        load.wait()

    def predict(pos, vel, force, jerk, e):
        pred_pos = pos + vel * e + force * (e * e / 2.0) + jerk * (e * e * e / 6.0)
        pred_vel = vel + force * e + jerk * (e * e / 2.0)
        return pred_pos, pred_vel

    def correct(pos, vel, force, jerk, new_force, new_jerk, e):
        half, twelfth = e / 2.0, e * e / 12.0
        new_vel = vel + (force + new_force) * half + (jerk - new_jerk) * twelfth
        new_pos = pos + (vel + new_vel) * half + (force - new_force) * twelfth
        return new_pos, new_vel

    def send(buffer, used, phase):
        copies = []
        for step in range(1, total):
            copy = pltpu.make_async_remote_copy(
                src_ref=buffer.at[0, pl.ds(0, used)],
                dst_ref=buffer.at[step, pl.ds(0, used)],
                send_sem=send_sem.at[phase, step],
                recv_sem=recv_sem.at[phase, step],
                device_id=peers[step],
                device_id_type=pl.DeviceIdType.MESH,
            )
            copy.start()
            copies.append(copy)
        return copies

    def stage_targets(buffer):
        for axis in range(6):
            line = jnp.broadcast_to(buffer[0, axis : axis + 1, :], (block, block))
            spread_t[axis] = jnp.transpose(line)

    def gather_forces(buffer, copies):
        acc[...] = jnp.zeros_like(acc)
        width = wave if total <= 64 else 8
        for lo in range(0, total, width):
            hi = min(lo + width, total)
            if buffer is second and hi == total:
                for copy in copies:
                    copy.wait_send()
            for step in range(max(lo, 1), hi):
                copies[step - 1].wait_recv()

            def tile(group, carry):
                at = pl.ds(pl.multiple_of(group * lane_tile, lane_tile), lane_tile)
                here = [spread_t[axis, at, :] for axis in range(6)]
                sums = [acc[axis, at, :] for axis in range(6)]
                for s in range(lo, hi):
                    r = [buffer[s, x : x + 1, :] - here[x] for x in range(3)]
                    w = [buffer[s, x + 3 : x + 4, :] - here[x + 3] for x in range(3)]
                    s2 = (r[0] * r[0] + r[1] * r[1]) + (r[2] * r[2] + soft_sq)
                    inv = lax.rsqrt(s2)
                    inv_sq = inv * inv
                    weight = (first[s, 6:7, :] * inv) * inv_sq
                    radial = ((r[0] * w[0] + r[1] * w[1]) + r[2] * w[2]) * (inv_sq * 3.0)
                    for x in range(3):
                        sums[x] = sums[x] + weight * r[x]
                        sums[x + 3] = sums[x + 3] + weight * (w[x] - radial * r[x])
                for axis in range(6):
                    acc[axis, at, :] = sums[axis]
                return carry

            lax.fori_loop(0, block // lane_tile, tile, 0, unroll=16 if total <= 64 else 1)
        sums = [
            jnp.sum(jnp.transpose(acc[axis]), axis=0, keepdims=True) for axis in range(6)
        ]
        return jnp.concatenate(sums[:3], axis=0), jnp.concatenate(sums[3:], axis=0)

    pos, vel, force, jerk = (part[3 * k : 3 * k + 3, :] for k in range(4))
    pred_pos, pred_vel = predict(pos, vel, force, jerk, step_time)
    first[0, 0:3, :] = pred_pos
    first[0, 3:6, :] = pred_vel
    first[0, 6:7, :] = mass[...] * mass_scale

    pl.semaphore_wait(barrier, total - 1)
    copies = send(first, 7, 0)

    slot = lax.broadcasted_iota(jnp.int32, (1, block), 1)
    kept = jnp.where(slot < count[...], order[...], -1)
    kept = jnp.transpose(jnp.broadcast_to(kept.astype(jnp.float32), (block, block)))
    name = lax.broadcasted_iota(jnp.int32, (block, block), 1).astype(jnp.float32)
    listed = jnp.sum(jnp.where(kept == name, 1.0, 0.0), axis=0, keepdims=True)
    on_first = jnp.where(level[...] == 0, listed, 0.0) > 0.5
    on_second = jnp.where(level[...] <= 1, listed, 0.0) > 0.5

    stage_targets(first)
    new_force, new_jerk = gather_forces(first, copies)
    new_pos, new_vel = correct(pos, vel, force, jerk, new_force, new_jerk, step_time)
    pos = jnp.where(on_first, new_pos, pos)
    vel = jnp.where(on_first, new_vel, vel)
    force = jnp.where(on_first, new_force, force)
    jerk = jnp.where(on_first, new_jerk, jerk)
    elapsed = jnp.where(on_first, step_time, 2.0 * step_time)

    pred_pos, pred_vel = predict(pos, vel, force, jerk, elapsed)
    second[0, 0:3, :] = pred_pos
    second[0, 3:6, :] = pred_vel
    later = send(second, 6, 1)
    stage_targets(second)
    for copy in copies:
        copy.wait_send()
    new_force, new_jerk = gather_forces(second, later)
    new_pos, new_vel = correct(pos, vel, force, jerk, new_force, new_jerk, elapsed)
    out_ref[0:3, :] = jnp.where(on_second, new_pos, pos)
    out_ref[3:6, :] = jnp.where(on_second, new_vel, vel)
    out_ref[6:9, :] = jnp.where(on_second, new_force, force)
    out_ref[9:12, :] = jnp.where(on_second, new_jerk, jerk)


def per_device(particles, masses, levels, counts, active_order):
    rows, cols = lax.axis_size("row"), lax.axis_size("col")
    total = rows * cols
    block = particles.shape[1]
    particle_total = block * total
    soft_sq = soft_coef * float(particle_total) ** (-2.0 / 3.0)
    f32 = jnp.float32
    return pl.pallas_call(
        functools.partial(kernel, rows, cols, soft_sq, 1.0 / float(particle_total)),
        out_shape=jax.ShapeDtypeStruct(particles.shape, f32),
        in_specs=[pl.BlockSpec(memory_space=pl.ANY)] * 5,
        out_specs=pl.BlockSpec(memory_space=pltpu.VMEM),
        scratch_shapes=[
            pltpu.VMEM(particles.shape, f32),
            pltpu.VMEM((1, block), f32),
            pltpu.VMEM((1, 1), jnp.int32),
            pltpu.VMEM((1, 1), jnp.int32),
            pltpu.VMEM((1, block), jnp.int32),
            pltpu.VMEM((total, 8, block), f32),
            pltpu.VMEM((total, 8, block), f32),
            pltpu.VMEM((6, block, block), f32),
            pltpu.VMEM((6, block, block), f32),
            pltpu.SemaphoreType.DMA((5,)),
            pltpu.SemaphoreType.DMA((2, total)),
            pltpu.SemaphoreType.DMA((2, total)),
        ],
        compiler_params=pltpu.CompilerParams(
            collective_id=0, has_side_effects=True, vmem_limit_bytes=vmem_grant
        ),
    )(*(pltpu.with_memory_space_constraint(a, pltpu.HBM) for a in (particles, masses.reshape(1, block))), levels.reshape(1, 1), counts.reshape(1, 1), pltpu.with_memory_space_constraint(active_order, pltpu.HBM))


def solution(mesh):
    in_specs = (
        P(None, ("row", "col")),
        P(("row", "col")),
        P(("row", "col")),
        P(("row", "col")),
        P(("row", "col"), None),
    )
    out_specs = P(None, ("row", "col"))
    return jax.shard_map(
        per_device, mesh=mesh, in_specs=in_specs, out_specs=out_specs, check_vma=False
    )
```

```python
import functools

import jax
import jax.numpy as jnp
from jax import lax
from jax.experimental import pallas as pl
from jax.experimental.pallas import tpu as pltpu
from jax.sharding import PartitionSpec as P

step_time = 0.5
soft_coef = 1.5
lane_tile = 8
wave = 2
vmem_grant = 16 * 1024 * 1024


def flip(index, mask):
    out = index
    bit = 1
    while bit <= mask:
        if mask & bit:
            out = out + bit * (1 - 2 * ((index // bit) % 2))
        bit *= 2
    return out


def shifted(index, offset, size):
    if size & (size - 1) == 0:
        return flip(index, offset)
    return lax.rem(index + offset, size)


def nearness(pair):
    dr, dc = pair
    return dr // 2 + dc % 2 + dc // 2, dr % 2


def kernel(
    rows, cols, soft_sq, mass_scale,
    part_hbm, mass_hbm, level_hbm, count_hbm, order_hbm, out_ref,
    part, mass, level, count, order, first, second, spread_t, acc,
    in_sem, send_sem, recv_sem,
):
    row, col = lax.axis_index("row"), lax.axis_index("col")
    total = rows * cols
    block = part.shape[1]
    offsets = sorted(
        ((dr, dc) for dr in range(rows) for dc in range(cols)), key=nearness
    )
    peers = [(shifted(row, dr, rows), shifted(col, dc, cols)) for dr, dc in offsets]

    loads = [
        pltpu.make_async_copy(src, dst, in_sem.at[i])
        for i, (src, dst) in enumerate(
            (
                (part_hbm, part),
                (mass_hbm, mass),
                (level_hbm, level),
                (count_hbm, count),
                (order_hbm, order),
            )
        )
    ]
    for load in loads:
        load.start()
    barrier = pltpu.get_barrier_semaphore()
    for peer in peers[:0:-1]:
        pl.semaphore_signal(
            barrier, inc=1, device_id=peer, device_id_type=pl.DeviceIdType.MESH
        )
    for load in loads:
        load.wait()

    def predict(pos, vel, force, jerk, e):
        pred_pos = pos + vel * e + force * (e * e / 2.0) + jerk * (e * e * e / 6.0)
        pred_vel = vel + force * e + jerk * (e * e / 2.0)
        return pred_pos, pred_vel

    def correct(pos, vel, force, jerk, new_force, new_jerk, e):
        half, twelfth = e / 2.0, e * e / 12.0
        new_vel = vel + (force + new_force) * half + (jerk - new_jerk) * twelfth
        new_pos = pos + (vel + new_vel) * half + (force - new_force) * twelfth
        return new_pos, new_vel

    def send(buffer, used, phase):
        copies = []
        for step in range(1, total):
            copy = pltpu.make_async_remote_copy(
                src_ref=buffer.at[0, pl.ds(0, used)],
                dst_ref=buffer.at[step, pl.ds(0, used)],
                send_sem=send_sem.at[phase, step],
                recv_sem=recv_sem.at[phase, step],
                device_id=peers[step],
                device_id_type=pl.DeviceIdType.MESH,
            )
            copy.start()
            copies.append(copy)
        return copies

    def stage_targets(buffer):
        for axis in range(6):
            line = jnp.broadcast_to(buffer[0, axis : axis + 1, :], (block, block))
            spread_t[axis] = jnp.transpose(line)

    def gather_forces(buffer, copies):
        acc[...] = jnp.zeros_like(acc)
        width = (1 if buffer is first else 2) if total <= 64 else 8
        for lo in range(0, total, width):
            hi = min(lo + width, total)
            if buffer is second and hi == total:
                for copy in copies:
                    copy.wait_send()
            for step in range(max(lo, 1), hi):
                copies[step - 1].wait_recv()

            def tile(group, carry):
                at = pl.ds(pl.multiple_of(group * lane_tile, lane_tile), lane_tile)
                here = [spread_t[axis, at, :] for axis in range(6)]
                sums = [acc[axis, at, :] for axis in range(6)]
                for s in range(lo, hi):
                    r = [buffer[s, x : x + 1, :] - here[x] for x in range(3)]
                    w = [buffer[s, x + 3 : x + 4, :] - here[x + 3] for x in range(3)]
                    s2 = (r[0] * r[0] + r[1] * r[1]) + (r[2] * r[2] + soft_sq)
                    inv = lax.rsqrt(s2)
                    inv_sq = inv * inv
                    weight = (first[s, 6:7, :] * inv) * inv_sq
                    radial = ((r[0] * w[0] + r[1] * w[1]) + r[2] * w[2]) * (inv_sq * 3.0)
                    for x in range(3):
                        sums[x] = sums[x] + weight * r[x]
                        sums[x + 3] = sums[x + 3] + weight * (w[x] - radial * r[x])
                for axis in range(6):
                    acc[axis, at, :] = sums[axis]
                return carry

            lax.fori_loop(0, block // lane_tile, tile, 0, unroll=16 if total <= 64 else 1)
        sums = [
            jnp.sum(jnp.transpose(acc[axis]), axis=0, keepdims=True) for axis in range(6)
        ]
        return jnp.concatenate(sums[:3], axis=0), jnp.concatenate(sums[3:], axis=0)

    pos, vel, force, jerk = (part[3 * k : 3 * k + 3, :] for k in range(4))
    pred_pos, pred_vel = predict(pos, vel, force, jerk, step_time)
    first[0, 0:3, :] = pred_pos
    first[0, 3:6, :] = pred_vel
    first[0, 6:7, :] = mass[...] * mass_scale

    pl.semaphore_wait(barrier, total - 1)
    copies = send(first, 7, 0)

    slot = lax.broadcasted_iota(jnp.int32, (1, block), 1)
    kept = jnp.where(slot < count[...], order[...], -1)
    kept = jnp.transpose(jnp.broadcast_to(kept.astype(jnp.float32), (block, block)))
    name = lax.broadcasted_iota(jnp.int32, (block, block), 1).astype(jnp.float32)
    listed = jnp.sum(jnp.where(kept == name, 1.0, 0.0), axis=0, keepdims=True)
    on_first = jnp.where(level[...] == 0, listed, 0.0) > 0.5
    on_second = jnp.where(level[...] <= 1, listed, 0.0) > 0.5

    stage_targets(first)
    new_force, new_jerk = gather_forces(first, copies)
    new_pos, new_vel = correct(pos, vel, force, jerk, new_force, new_jerk, step_time)
    pos = jnp.where(on_first, new_pos, pos)
    vel = jnp.where(on_first, new_vel, vel)
    force = jnp.where(on_first, new_force, force)
    jerk = jnp.where(on_first, new_jerk, jerk)
    elapsed = jnp.where(on_first, step_time, 2.0 * step_time)

    pred_pos, pred_vel = predict(pos, vel, force, jerk, elapsed)
    second[0, 0:3, :] = pred_pos
    second[0, 3:6, :] = pred_vel
    later = send(second, 6, 1)
    stage_targets(second)
    for copy in copies:
        copy.wait_send()
    new_force, new_jerk = gather_forces(second, later)
    new_pos, new_vel = correct(pos, vel, force, jerk, new_force, new_jerk, elapsed)
    out_ref[0:3, :] = jnp.where(on_second, new_pos, pos)
    out_ref[3:6, :] = jnp.where(on_second, new_vel, vel)
    out_ref[6:9, :] = jnp.where(on_second, new_force, force)
    out_ref[9:12, :] = jnp.where(on_second, new_jerk, jerk)


def per_device(particles, masses, levels, counts, active_order):
    rows, cols = lax.axis_size("row"), lax.axis_size("col")
    total = rows * cols
    block = particles.shape[1]
    particle_total = block * total
    soft_sq = soft_coef * float(particle_total) ** (-2.0 / 3.0)
    f32 = jnp.float32
    return pl.pallas_call(
        functools.partial(kernel, rows, cols, soft_sq, 1.0 / float(particle_total)),
        out_shape=jax.ShapeDtypeStruct(particles.shape, f32),
        in_specs=[pl.BlockSpec(memory_space=pl.ANY)] * 5,
        out_specs=pl.BlockSpec(memory_space=pltpu.VMEM),
        scratch_shapes=[
            pltpu.VMEM(particles.shape, f32),
            pltpu.VMEM((1, block), f32),
            pltpu.VMEM((1, 1), jnp.int32),
            pltpu.VMEM((1, 1), jnp.int32),
            pltpu.VMEM((1, block), jnp.int32),
            pltpu.VMEM((total, 8, block), f32),
            pltpu.VMEM((total, 8, block), f32),
            pltpu.VMEM((6, block, block), f32),
            pltpu.VMEM((6, block, block), f32),
            pltpu.SemaphoreType.DMA((5,)),
            pltpu.SemaphoreType.DMA((2, total)),
            pltpu.SemaphoreType.DMA((2, total)),
        ],
        compiler_params=pltpu.CompilerParams(
            collective_id=0, has_side_effects=True, vmem_limit_bytes=vmem_grant
        ),
    )(*(pltpu.with_memory_space_constraint(a, pltpu.HBM) for a in (particles, masses.reshape(1, block))), levels.reshape(1, 1), counts.reshape(1, 1), pltpu.with_memory_space_constraint(active_order, pltpu.HBM))


def solution(mesh):
    in_specs = (
        P(None, ("row", "col")),
        P(("row", "col")),
        P(("row", "col")),
        P(("row", "col")),
        P(("row", "col"), None),
    )
    out_specs = P(None, ("row", "col"))
    return jax.shard_map(
        per_device, mesh=mesh, in_specs=in_specs, out_specs=out_specs, check_vma=False
    )
```

```python
import functools

import jax
import jax.numpy as jnp
from jax import lax
from jax.experimental import pallas as pl
from jax.experimental.pallas import tpu as pltpu
from jax.sharding import PartitionSpec as P

step_time = 0.5
soft_coef = 1.5
lane_tile = 8
wave = 2
vmem_grant = 16 * 1024 * 1024


def flip(index, mask):
    out = index
    bit = 1
    while bit <= mask:
        if mask & bit:
            out = out + bit * (1 - 2 * ((index // bit) % 2))
        bit *= 2
    return out


def shifted(index, offset, size):
    if size & (size - 1) == 0:
        return flip(index, offset)
    return lax.rem(index + offset, size)


def nearness(pair):
    dr, dc = pair
    return dr // 2 + dc % 2 + dc // 2, dr % 2


def kernel(
    rows, cols, soft_sq, mass_scale,
    part_hbm, mass_hbm, level_hbm, count_hbm, order_hbm, out_ref,
    part, mass, level, count, order, first, second, spread_t, acc,
    in_sem, send_sem, recv_sem,
):
    row, col = lax.axis_index("row"), lax.axis_index("col")
    total = rows * cols
    block = part.shape[1]
    offsets = sorted(
        ((dr, dc) for dr in range(rows) for dc in range(cols)), key=nearness
    )
    peers = [(shifted(row, dr, rows), shifted(col, dc, cols)) for dr, dc in offsets]

    loads = [
        pltpu.make_async_copy(src, dst, in_sem.at[i])
        for i, (src, dst) in enumerate(
            (
                (part_hbm, part),
                (mass_hbm, mass),
                (level_hbm, level),
                (count_hbm, count),
                (order_hbm, order),
            )
        )
    ]
    for load in loads:
        load.start()
    barrier = pltpu.get_barrier_semaphore()
    for peer in peers[:0:-1]:
        pl.semaphore_signal(
            barrier, inc=1, device_id=peer, device_id_type=pl.DeviceIdType.MESH
        )
    for load in loads[:2]:
        load.wait()

    def predict(pos, vel, force, jerk, e):
        pred_pos = pos + vel * e + force * (e * e / 2.0) + jerk * (e * e * e / 6.0)
        pred_vel = vel + force * e + jerk * (e * e / 2.0)
        return pred_pos, pred_vel

    def correct(pos, vel, force, jerk, new_force, new_jerk, e):
        half, twelfth = e / 2.0, e * e / 12.0
        new_vel = vel + (force + new_force) * half + (jerk - new_jerk) * twelfth
        new_pos = pos + (vel + new_vel) * half + (force - new_force) * twelfth
        return new_pos, new_vel

    def send(buffer, used, phase):
        copies = []
        for step in range(1, total):
            copy = pltpu.make_async_remote_copy(
                src_ref=buffer.at[0, pl.ds(0, used)],
                dst_ref=buffer.at[step, pl.ds(0, used)],
                send_sem=send_sem.at[phase, step],
                recv_sem=recv_sem.at[phase, step],
                device_id=peers[step],
                device_id_type=pl.DeviceIdType.MESH,
            )
            copy.start()
            copies.append(copy)
        return copies

    def stage_targets(buffer):
        for axis in range(6):
            line = jnp.broadcast_to(buffer[0, axis : axis + 1, :], (block, block))
            spread_t[axis] = jnp.transpose(line)

    def gather_forces(buffer, copies):
        acc[...] = jnp.zeros_like(acc)
        width = wave if total <= 64 else 8
        for lo in range(0, total, width):
            hi = min(lo + width, total)
            if buffer is second and hi == total:
                for copy in copies:
                    copy.wait_send()
            for step in range(max(lo, 1), hi):
                copies[step - 1].wait_recv()

            def tile(group, carry):
                at = pl.ds(pl.multiple_of(group * lane_tile, lane_tile), lane_tile)
                here = [spread_t[axis, at, :] for axis in range(6)]
                sums = [acc[axis, at, :] for axis in range(6)]
                for s in range(lo, hi):
                    r = [buffer[s, x : x + 1, :] - here[x] for x in range(3)]
                    w = [buffer[s, x + 3 : x + 4, :] - here[x + 3] for x in range(3)]
                    s2 = (r[0] * r[0] + r[1] * r[1]) + (r[2] * r[2] + soft_sq)
                    inv = lax.rsqrt(s2)
                    inv_sq = inv * inv
                    weight = (first[s, 6:7, :] * inv) * inv_sq
                    radial = ((r[0] * w[0] + r[1] * w[1]) + r[2] * w[2]) * (inv_sq * 3.0)
                    for x in range(3):
                        sums[x] = sums[x] + weight * r[x]
                        sums[x + 3] = sums[x + 3] + weight * (w[x] - radial * r[x])
                for axis in range(6):
                    acc[axis, at, :] = sums[axis]
                return carry

            lax.fori_loop(0, block // lane_tile, tile, 0, unroll=16 if total <= 64 else 1)
        sums = [
            jnp.sum(jnp.transpose(acc[axis]), axis=0, keepdims=True) for axis in range(6)
        ]
        return jnp.concatenate(sums[:3], axis=0), jnp.concatenate(sums[3:], axis=0)

    pos, vel, force, jerk = (part[3 * k : 3 * k + 3, :] for k in range(4))
    pred_pos, pred_vel = predict(pos, vel, force, jerk, step_time)
    first[0, 0:3, :] = pred_pos
    first[0, 3:6, :] = pred_vel
    first[0, 6:7, :] = mass[...] * mass_scale

    pl.semaphore_wait(barrier, total - 1)
    copies = send(first, 7, 0)
    for load in loads[2:]:
        load.wait()

    slot = lax.broadcasted_iota(jnp.int32, (1, block), 1)
    kept = jnp.where(slot < count[...], order[...], -1)
    kept = jnp.transpose(jnp.broadcast_to(kept.astype(jnp.float32), (block, block)))
    name = lax.broadcasted_iota(jnp.int32, (block, block), 1).astype(jnp.float32)
    listed = jnp.sum(jnp.where(kept == name, 1.0, 0.0), axis=0, keepdims=True)
    on_first = jnp.where(level[...] == 0, listed, 0.0) > 0.5
    on_second = jnp.where(level[...] <= 1, listed, 0.0) > 0.5

    stage_targets(first)
    new_force, new_jerk = gather_forces(first, copies)
    new_pos, new_vel = correct(pos, vel, force, jerk, new_force, new_jerk, step_time)
    pos = jnp.where(on_first, new_pos, pos)
    vel = jnp.where(on_first, new_vel, vel)
    force = jnp.where(on_first, new_force, force)
    jerk = jnp.where(on_first, new_jerk, jerk)
    elapsed = jnp.where(on_first, step_time, 2.0 * step_time)

    pred_pos, pred_vel = predict(pos, vel, force, jerk, elapsed)
    second[0, 0:3, :] = pred_pos
    second[0, 3:6, :] = pred_vel
    later = send(second, 6, 1)
    stage_targets(second)
    for copy in copies:
        copy.wait_send()
    new_force, new_jerk = gather_forces(second, later)
    new_pos, new_vel = correct(pos, vel, force, jerk, new_force, new_jerk, elapsed)
    out_ref[0:3, :] = jnp.where(on_second, new_pos, pos)
    out_ref[3:6, :] = jnp.where(on_second, new_vel, vel)
    out_ref[6:9, :] = jnp.where(on_second, new_force, force)
    out_ref[9:12, :] = jnp.where(on_second, new_jerk, jerk)


def per_device(particles, masses, levels, counts, active_order):
    rows, cols = lax.axis_size("row"), lax.axis_size("col")
    total = rows * cols
    block = particles.shape[1]
    particle_total = block * total
    soft_sq = soft_coef * float(particle_total) ** (-2.0 / 3.0)
    f32 = jnp.float32
    return pl.pallas_call(
        functools.partial(kernel, rows, cols, soft_sq, 1.0 / float(particle_total)),
        out_shape=jax.ShapeDtypeStruct(particles.shape, f32),
        in_specs=[pl.BlockSpec(memory_space=pl.ANY)] * 5,
        out_specs=pl.BlockSpec(memory_space=pltpu.VMEM),
        scratch_shapes=[
            pltpu.VMEM(particles.shape, f32),
            pltpu.VMEM((1, block), f32),
            pltpu.VMEM((1, 1), jnp.int32),
            pltpu.VMEM((1, 1), jnp.int32),
            pltpu.VMEM((1, block), jnp.int32),
            pltpu.VMEM((total, 8, block), f32),
            pltpu.VMEM((total, 8, block), f32),
            pltpu.VMEM((6, block, block), f32),
            pltpu.VMEM((6, block, block), f32),
            pltpu.SemaphoreType.DMA((5,)),
            pltpu.SemaphoreType.DMA((2, total)),
            pltpu.SemaphoreType.DMA((2, total)),
        ],
        compiler_params=pltpu.CompilerParams(
            collective_id=0, has_side_effects=True, vmem_limit_bytes=vmem_grant
        ),
    )(*(pltpu.with_memory_space_constraint(a, pltpu.HBM) for a in (particles, masses.reshape(1, block))), levels.reshape(1, 1), counts.reshape(1, 1), pltpu.with_memory_space_constraint(active_order, pltpu.HBM))


def solution(mesh):
    in_specs = (
        P(None, ("row", "col")),
        P(("row", "col")),
        P(("row", "col")),
        P(("row", "col")),
        P(("row", "col"), None),
    )
    out_specs = P(None, ("row", "col"))
    return jax.shard_map(
        per_device, mesh=mesh, in_specs=in_specs, out_specs=out_specs, check_vma=False
    )
```
